256 devices in a mesh: cells: 32 (over z, y), genes: 8 (over x, core).
Axes of the slice: x: 4, y: 4, z: 8, core: 2. Of those that a mesh axis runs over, the one named last changes fastest.
Arguments:
- tiles: bfloat16 [32, 8, 16, 512, 512], P('cells', 'genes'), may hold values from -0.25 to 0.25
- tile_row: int32 [32, 8, 16], P('cells', 'genes'), may hold values from 0 to 7, as said below
- tile_col: int32 [32, 8, 16], P('cells', 'genes'), may hold values from 0 to 7, as said below
- tile_count: int32 [32, 8], P('cells', 'genes'), may hold values from 2 to 16, as said below
- sketch: bfloat16 [32768, 128], P(('genes', 'cells')), may hold values from -3 to 3
Outputs:
- projected: bfloat16 [131072, 128], P('cells')
- back: float32 [32768, 128], P(('genes', 'cells'))
The draws below stay inside these ranges and needn't reach their ends.
Inputs may be any that keep to these rules, and one draw needn't show every extreme that they name: Slot s of a device holds the tile at this tile row of the device's cell slab; the (tile_row, tile_col) positions of one device's 16 slots are all different. `tile_col`: slot s of a device holds the tile at this tile column of the device's gene block. Slots tile_count and beyond hold no part of the matrix; some device in every draw has all 16 slots live.
All inputs are finite; a program needn't handle non-finite values.
Results may differ from the reference program's by a relative error of at most 0.011.
Values may be sent and summed in bfloat16 or wider, within the bound.
No kernel may reach another device: no remote copies, remote signals or barrier semaphores. Data moves between devices by JAX's collectives and lax.ppermute only.
A program may use at most 64 MiB of HBM per device.

```python
import math
import jax
import jax.numpy as jnp
from jax import lax

TILE_EDGE = 512
GENES = 32768
SKETCH = 128
SLOTS = 16
SLAB_TILES = 8
COL_TILES = 8
CELLS = 131072
COL_LOAD = 32
N_CELLS = 32
N_GENES = 8


def tile_positions(key):
    base = jax.random.fold_in(key, 7)
    key_list = jax.random.split(base, N_CELLS * N_GENES)
    orders = jax.vmap(lambda single: jax.random.permutation(single, SLAB_TILES * COL_TILES))(key_list)
    return orders[:, :SLOTS].reshape(N_CELLS, N_GENES, SLOTS).astype(jnp.int32)


def draw_tile_row(key, part):
    return (tile_positions(key) // COL_TILES).astype(jnp.int32)


def draw_tile_col(key, part):
    return (tile_positions(key) % COL_TILES).astype(jnp.int32)


def draw_tile_count(key, part):
    base = jax.random.fold_in(key, 11)
    first_key, second_key, third_key = jax.random.split(base, 3)
    first = jax.random.randint(first_key, (N_CELLS * N_GENES,), 0, SLOTS - 1)
    second = jax.random.randint(second_key, (N_CELLS * N_GENES,), 0, SLOTS - 1)
    counts = 2 + first * second // (SLOTS - 2)
    busiest = jax.random.randint(third_key, (), 0, N_CELLS * N_GENES)
    counts = jnp.where(jnp.arange(N_CELLS * N_GENES) == busiest, SLOTS, counts)
    return counts.reshape(N_CELLS, N_GENES).astype(jnp.int32)


def levels(stream_key, extent, cuts, low, top_value):
    factor_of = 1.0
    for position, parts in cuts:
        heights = jax.random.uniform(jax.random.fold_in(jax.random.fold_in(stream_key, 6), position), (parts,), jnp.float32, low / len(cuts), top_value / len(cuts))
        factor_of = factor_of * jnp.repeat(jnp.exp(heights), extent[position] // parts).reshape((-1,) + (1,) * (len(extent) - 1 - position))
    return factor_of


def noise(own_key, extent, scale, bound, shards=(), dtype=jnp.bfloat16):
    gain = levels(own_key, extent, shards, -0.22, 0.18) if shards else 1.0
    values = jax.random.normal(own_key, extent, jnp.float32) * scale * gain
    return jnp.minimum(jnp.maximum(values, -bound), bound).astype(dtype)


def setup_inputs(seed: int = 0) -> dict:
    keys = jax.random.split(jax.random.key(seed), 6)
    return {
        "tiles": noise(keys[0], (N_CELLS, N_GENES, SLOTS, TILE_EDGE, TILE_EDGE), TILE_EDGE ** -0.5, 0.25, ((0, 32), (1, 8))),
        "tile_row": draw_tile_row(jax.random.fold_in(keys[5], 71), 0),
        "tile_col": draw_tile_col(jax.random.fold_in(keys[5], 71), 0),
        "tile_count": draw_tile_count(jax.random.fold_in(keys[5], 71), 0),
        "sketch": noise(keys[4], (GENES, SKETCH), 0.5, 3.0, ((0, 256),)),
    }


def forward_block(blocks, rows, cols, count, sketch_tiles):
    live = jnp.arange(SLOTS) < count
    col_pick = (cols[:, None] == jnp.arange(COL_TILES)[None, :]).astype(jnp.float32)
    picked = jnp.einsum('sc,cik->sik', col_pick, sketch_tiles, precision=lax.Precision.HIGHEST)
    products = jnp.einsum('sij,sjk->sik', blocks.astype(jnp.float32), picked, precision=lax.Precision.HIGHEST)
    row_pick = ((rows[:, None] == jnp.arange(SLAB_TILES)[None, :]) & live[:, None]).astype(jnp.float32)
    return jnp.einsum('sr,sik->rik', row_pick, products, precision=lax.Precision.HIGHEST)

def backward_block(blocks, rows, cols, count, slab_rows):
    live = jnp.arange(SLOTS) < count
    row_pick = (rows[:, None] == jnp.arange(SLAB_TILES)[None, :]).astype(jnp.float32)
    picked = jnp.einsum('sr,rik->sik', row_pick, slab_rows, precision=lax.Precision.HIGHEST)
    products = jnp.einsum('sij,sik->sjk', blocks.astype(jnp.float32), picked, precision=lax.Precision.HIGHEST)
    col_pick = ((cols[:, None] == jnp.arange(COL_TILES)[None, :]) & live[:, None]).astype(jnp.float32)
    return jnp.einsum('sc,sjk->cjk', col_pick, products, precision=lax.Precision.HIGHEST)

def reference(tiles, tile_row, tile_col, tile_count, sketch):
    sketch_all = sketch.astype(jnp.float32).reshape(N_GENES, COL_TILES, TILE_EDGE, SKETCH)

    def slab_sum(cell_id):

        def one_block(gene_id):
            return forward_block(tiles[cell_id, gene_id], tile_row[cell_id, gene_id], tile_col[cell_id, gene_id], tile_count[cell_id, gene_id], sketch_all[gene_id])
        return lax.optimization_barrier(jnp.sum(lax.map(one_block, jnp.arange(N_GENES)), axis=0))
    summed = lax.map(slab_sum, jnp.arange(N_CELLS))
    projected = summed.astype(jnp.bfloat16).reshape(CELLS, SKETCH)
    slabs = projected.astype(jnp.float32).reshape(N_CELLS, SLAB_TILES, TILE_EDGE, SKETCH)

    def column_sum(gene_id):

        def one_block(cell_id):
            return backward_block(tiles[cell_id, gene_id], tile_row[cell_id, gene_id], tile_col[cell_id, gene_id], tile_count[cell_id, gene_id], slabs[cell_id])
        return lax.optimization_barrier(jnp.sum(lax.map(one_block, jnp.arange(N_CELLS)), axis=0))
    columns = lax.map(column_sum, jnp.arange(N_GENES)).reshape(GENES, SKETCH)
    back = columns * (1.0 / math.sqrt(COL_LOAD))
    return (projected, back)
```

```python
import functools
import math

import jax
import jax.numpy as jnp
from jax import lax
from jax.experimental import pallas as pl
from jax.experimental.pallas import tpu as pltpu
from jax.sharding import PartitionSpec as P


NZ, NY, NX, NC = 8, 4, 4, 2
SLOTS, EDGE, WIDTH, ROWS, COLS = 16, 512, 128, 8, 8
F32, BF16 = jnp.float32, jnp.bfloat16
VMEM = pl.BlockSpec(memory_space=pltpu.VMEM)
SMEM = pl.BlockSpec(memory_space=pltpu.SMEM)
HBM = pl.BlockSpec(memory_space=pl.ANY)


def where_am_i():
    cell, gene = lax.axis_index("cells"), lax.axis_index("genes")
    return cell // NY, cell % NY, gene // NC, gene % NC


def z_shift(v, k):
    return lax.ppermute(v, "cells", [(z * NY + y, (z + k) % NZ * NY + y) for z in range(NZ) for y in range(NY)])


def y_shift(v, k):
    return lax.ppermute(v, "cells", [(z * NY + y, z * NY + (y + k) % NY) for z in range(NZ) for y in range(NY)])


def x_shift(v, k):
    return lax.ppermute(v, "genes", [(x * NC + c, (x + k) % NX * NC + c) for x in range(NX) for c in range(NC)])


def core_swap(v):
    return lax.ppermute(v, "genes", [(x * NC + c, x * NC + 1 - c) for x in range(NX) for c in range(NC)])


def shape(dims, dtype):
    return jax.ShapeDtypeStruct(dims, dtype)


def tile_copy(tiles, held, sems, s):
    return pltpu.make_async_copy(tiles.at[s], held.at[s], sems.at[s])


def start_tiles(count, tiles, held, sems):
    for s in range(SLOTS):
        @pl.when(s < count)
        def _():
            tile_copy(tiles, held, sems, s).start()


def forward_kernel(rows, cols, counts, tiles, *refs):
    gathered, (keep, send, held, sketch, total, sems) = refs[:NY], refs[NY:]
    z, y, x, c = where_am_i()
    count = counts[0]
    start_tiles(count, tiles, held, sems)
    for m in range(NY):
        part = lax.rem(y - m + NY, NY)
        for k in range(NZ):
            tile = lax.rem(z - k + NZ, NZ)
            sketch[tile, pl.ds(pl.multiple_of(part * WIDTH, WIDTH), WIDTH), :] = gathered[m][k]
    total[...] = jnp.zeros_like(total)

    def step(s, _):
        tile_copy(tiles, held, sems, s).wait()
        r = rows[s]
        total[r] += jnp.dot(held[s], sketch[cols[s]], preferred_element_type=F32)
        return 0

    lax.fori_loop(0, count, step, 0)
    for k in range(NX):
        owner = lax.rem(x + k, NX)
        keep[k] = total[c * NX + owner]
        send[k] = total[(1 - c) * NX + owner].astype(BF16)


def forward(rows, cols, counts, tiles, gathered):
    return pl.pallas_call(
        forward_kernel,
        out_shape=(shape((NX, EDGE, WIDTH), F32), shape((NX, EDGE, WIDTH), BF16)),
        in_specs=[SMEM, SMEM, SMEM, HBM] + [VMEM] * NY,
        out_specs=(VMEM, VMEM),
        scratch_shapes=[
            pltpu.VMEM((SLOTS, EDGE, EDGE), BF16),
            pltpu.VMEM((COLS, EDGE, WIDTH), BF16),
            pltpu.VMEM((ROWS, EDGE, WIDTH), F32),
            pltpu.SemaphoreType.DMA((SLOTS,)),
        ],
        compiler_params=pltpu.CompilerParams(vmem_limit_bytes=24 << 20),
        name="forward",
    )(rows, cols, counts, tiles, *gathered)


def pair_kernel(keep, other, own, *sends):
    own[...] = keep[0] + other[0].astype(F32)
    for k, out in enumerate(sends, 1):
        out[...] = (keep[k] + other[k].astype(F32)).astype(BF16)


def pair_sum(keep, other):
    return pl.pallas_call(
        pair_kernel,
        out_shape=(shape((EDGE, WIDTH), F32),) + (shape((EDGE, WIDTH), BF16),) * (NX - 1),
        in_specs=[VMEM, VMEM],
        out_specs=(VMEM,) * NX,
        compiler_params=pltpu.CompilerParams(vmem_limit_bytes=8 << 20),
        name="pair_sum",
    )(keep, other)


def share_kernel(own, *refs):
    refs[-1][...] = (own[...] + sum(r[...].astype(F32) for r in refs[:-1])).astype(BF16)


def share_sum(own, arrived):
    return pl.pallas_call(
        share_kernel,
        out_shape=shape((EDGE, WIDTH), BF16),
        in_specs=[VMEM] * NX,
        out_specs=VMEM,
        compiler_params=pltpu.CompilerParams(vmem_limit_bytes=4 << 20),
        name="share_sum",
    )(own, *arrived)


def backward_kernel(rows, cols, counts, tiles, *refs):
    mine, theirs = refs[:NX], refs[NX : 2 * NX]
    projected, own = refs[2 * NX], refs[2 * NX + 1]
    sends = refs[2 * NX + 2 : 2 * NX + 1 + NY]
    held, turned, total, sems = refs[2 * NX + 1 + NY :]
    z, y, x, c = where_am_i()
    count = counts[0]
    start_tiles(count, tiles, held, sems)
    total[...] = jnp.zeros_like(total)
    for k in range(NX):
        owner = lax.rem(x - k + NX, NX)
        for core, part in ((c, mine[k]), (1 - c, theirs[k])):
            r = core * NX + owner
            value = part[...]
            projected[pl.ds(pl.multiple_of(r * EDGE, EDGE), EDGE), :] = value
            turned[r] = value.T

    def step(s, _):
        tile_copy(tiles, held, sems, s).wait()
        product = jnp.dot(turned[rows[s]], held[s], preferred_element_type=F32)
        col = cols[s]
        for j in range(NY):
            total[col, j] += product[:, j * WIDTH : (j + 1) * WIDTH]
        return 0

    lax.fori_loop(0, count, step, 0)
    for k in range(NZ):
        tile = lax.rem(z + k, NZ)
        own[k] = total[tile, y]
        for m in range(1, NY):
            sends[m - 1][k] = total[tile, lax.rem(y + m, NY)].astype(BF16)


def backward(rows, cols, counts, tiles, mine, theirs):
    block = (NZ, WIDTH, WIDTH)
    return pl.pallas_call(
        backward_kernel,
        out_shape=(shape((ROWS * EDGE, WIDTH), BF16), shape(block, F32)) + (shape(block, BF16),) * (NY - 1),
        in_specs=[SMEM, SMEM, SMEM, HBM] + [VMEM] * (2 * NX),
        out_specs=(VMEM,) * (NY + 1),
        scratch_shapes=[
            pltpu.VMEM((SLOTS, EDGE, EDGE), BF16),
            pltpu.VMEM((ROWS, WIDTH, EDGE), BF16),
            pltpu.VMEM((COLS, NY, WIDTH, WIDTH), F32),
            pltpu.SemaphoreType.DMA((SLOTS,)),
        ],
        compiler_params=pltpu.CompilerParams(vmem_limit_bytes=24 << 20),
        name="backward",
    )(rows, cols, counts, tiles, *mine, *theirs)


def column_kernel(own, *refs):
    arrived, outs = refs[: NY - 1], refs[NY - 1 :]
    for k in range(NZ):
        value = own[k] + sum(r[k].astype(F32) for r in arrived)
        outs[k][...] = value.astype(outs[k].dtype)


def column_sum(own, arrived):
    block = (WIDTH, WIDTH)
    return pl.pallas_call(
        column_kernel,
        out_shape=(shape(block, F32),) + (shape(block, BF16),) * (NZ - 1),
        in_specs=[VMEM] * NY,
        out_specs=(VMEM,) * NZ,
        compiler_params=pltpu.CompilerParams(vmem_limit_bytes=8 << 20),
        name="column_sum",
    )(own, *arrived)


def last_kernel(scale, own, *refs):
    total = own[...] + sum(r[...].astype(F32) for r in refs[:-1])
    refs[-1][...] = total.T * scale


def last_sum(own, arrived, scale):
    return pl.pallas_call(
        functools.partial(last_kernel, scale),
        out_shape=shape((WIDTH, WIDTH), F32),
        in_specs=[VMEM] * NZ,
        out_specs=VMEM,
        compiler_params=pltpu.CompilerParams(vmem_limit_bytes=4 << 20),
        name="last_sum",
    )(own, *arrived)


def local(tiles, tile_row, tile_col, tile_count, sketch):
    tiles = tiles.reshape(SLOTS, EDGE, EDGE)
    rows, cols, counts = tile_row.reshape(SLOTS), tile_col.reshape(SLOTS), tile_count.reshape(1)
    along_z = jnp.stack([sketch] + [z_shift(sketch, k) for k in range(1, NZ)])
    gathered = [along_z] + [y_shift(along_z, m) for m in range(1, NY)]
    keep, send = forward(rows, cols, counts, tiles, gathered)
    own, *sends = pair_sum(keep, core_swap(send))
    share = share_sum(own, [x_shift(v, k) for k, v in enumerate(sends, 1)])
    mine = [share] + [x_shift(share, k) for k in range(1, NX)]
    theirs = [core_swap(v) for v in mine]
    projected, own, *sends = backward(rows, cols, counts, tiles, mine, theirs)
    own, *sends = column_sum(own, [y_shift(v, m) for m, v in enumerate(sends, 1)])
    load = max(1, lax.axis_size("cells") * SLOTS // (2 * COLS))
    back = last_sum(own, [z_shift(v, k) for k, v in enumerate(sends, 1)], 1.0 / math.sqrt(load))
    return projected, back


def solution(mesh):
    return jax.shard_map(
        local,
        mesh=mesh,
        in_specs=(
            P("cells", "genes", None, None, None),
            P("cells", "genes", None),
            P("cells", "genes", None),
            P("cells", "genes"),
            P(("genes", "cells"), None),
        ),
        out_specs=(P("cells", None), P(("genes", "cells"), None)),
        check_vma=False,
    )
```

```python
import functools
import math

import jax
import jax.numpy as jnp
from jax import lax
from jax.experimental import pallas as pl
from jax.experimental.pallas import tpu as pltpu
from jax.sharding import PartitionSpec as P


NZ, NY, NX, NC = 8, 4, 4, 2
SLOTS, EDGE, WIDTH, ROWS, COLS = 16, 512, 128, 8, 8
F32, BF16 = jnp.float32, jnp.bfloat16
VMEM = pl.BlockSpec(memory_space=pltpu.VMEM)
SMEM = pl.BlockSpec(memory_space=pltpu.SMEM)
HBM = pl.BlockSpec(memory_space=pl.ANY)


def where_am_i():
    cell, gene = lax.axis_index("cells"), lax.axis_index("genes")
    return cell // NY, cell % NY, gene // NC, gene % NC


def z_swap(v, k):
    return lax.ppermute(v, "cells", [(z * NY + y, (z ^ k) * NY + y) for z in range(NZ) for y in range(NY)])


def y_swap(v, k):
    return lax.ppermute(v, "cells", [(z * NY + y, z * NY + (y ^ k)) for z in range(NZ) for y in range(NY)])


def x_swap(v, k):
    return lax.ppermute(v, "genes", [(x * NC + c, (x ^ k) * NC + c) for x in range(NX) for c in range(NC)])


def core_swap(v):
    return lax.ppermute(v, "genes", [(x * NC + c, x * NC + 1 - c) for x in range(NX) for c in range(NC)])


def shape(dims, dtype):
    return jax.ShapeDtypeStruct(dims, dtype)


def fetch_kernel(counts, tiles, held, sems):
    count = counts[0]
    for go in (True, False):
        for s in range(SLOTS):
            @pl.when(s < count)
            def _():
                copy = pltpu.make_async_copy(tiles.at[s], held.at[s], sems.at[s])
                copy.start() if go else copy.wait()


def fetch(counts, tiles):
    return pl.pallas_call(
        fetch_kernel,
        out_shape=shape((SLOTS, EDGE, EDGE), BF16),
        in_specs=[SMEM, HBM],
        out_specs=VMEM,
        scratch_shapes=[pltpu.SemaphoreType.DMA((SLOTS,))],
        compiler_params=pltpu.CompilerParams(vmem_limit_bytes=12 << 20),
        name="fetch",
    )(counts, tiles)


def over_slots(count, body):
    def step(i, _):
        body(2 * i, 2 * i + 1, 2 * i + 1 < count)
        return 0

    lax.fori_loop(0, (count + 1) // 2, step, 0)


def forward_kernel(rows, cols, counts, held, *refs):
    gathered, (keep, send, sketch, total) = refs[:NY], refs[NY:]
    z, y, x, c = where_am_i()
    for m in range(NY):
        part = pl.ds(pl.multiple_of((y ^ m) * WIDTH, WIDTH), WIDTH)
        for k in range(NZ):
            sketch[z ^ k, part, :] = gathered[m][k]
    total[...] = jnp.zeros_like(total)

    def body(s, t, live):
        first = jnp.dot(held[s], sketch[cols[s]], preferred_element_type=F32)
        second = jnp.dot(held[t], sketch[cols[t]], preferred_element_type=F32)
        total[rows[s]] += first
        total[rows[t]] += jnp.where(live, second, 0.0)

    over_slots(counts[0], body)
    for k in range(NX):
        keep[k] = total[c * NX + (x ^ k)]
        send[k] = total[(1 - c) * NX + (x ^ k)].astype(BF16)


def forward(rows, cols, counts, held, gathered):
    return pl.pallas_call(
        forward_kernel,
        out_shape=(shape((NX, EDGE, WIDTH), F32), shape((NX, EDGE, WIDTH), BF16)),
        in_specs=[SMEM, SMEM, SMEM] + [VMEM] * (NY + 1),
        out_specs=(VMEM, VMEM),
        scratch_shapes=[
            pltpu.VMEM((COLS, EDGE, WIDTH), BF16),
            pltpu.VMEM((ROWS, EDGE, WIDTH), F32),
        ],
        compiler_params=pltpu.CompilerParams(vmem_limit_bytes=24 << 20),
        name="forward",
    )(rows, cols, counts, held, *gathered)


def pair_kernel(keep, other, own, *sends):
    own[...] = keep[0] + other[0].astype(F32)
    for k, out in enumerate(sends, 1):
        out[...] = (keep[k] + other[k].astype(F32)).astype(BF16)


def pair_sum(keep, other):
    return pl.pallas_call(
        pair_kernel,
        out_shape=(shape((EDGE, WIDTH), F32),) + (shape((EDGE, WIDTH), BF16),) * (NX - 1),
        in_specs=[VMEM, VMEM],
        out_specs=(VMEM,) * NX,
        compiler_params=pltpu.CompilerParams(vmem_limit_bytes=8 << 20),
        name="pair_sum",
    )(keep, other)


def share_kernel(own, *refs):
    refs[-1][...] = (own[...] + sum(r[...].astype(F32) for r in refs[:-1])).astype(BF16)


def share_sum(own, arrived):
    return pl.pallas_call(
        share_kernel,
        out_shape=shape((EDGE, WIDTH), BF16),
        in_specs=[VMEM] * NX,
        out_specs=VMEM,
        compiler_params=pltpu.CompilerParams(vmem_limit_bytes=4 << 20),
        name="share_sum",
    )(own, *arrived)


def backward_kernel(rows, cols, counts, held, *refs):
    mine, theirs = refs[:NX], refs[NX : 2 * NX]
    projected, own = refs[2 * NX], refs[2 * NX + 1]
    sends = refs[2 * NX + 2 : 2 * NX + 1 + NY]
    turned, total = refs[2 * NX + 1 + NY :]
    z, y, x, c = where_am_i()
    total[...] = jnp.zeros_like(total)
    for k in range(NX):
        for core, part in ((c, mine[k]), (1 - c, theirs[k])):
            r = core * NX + (x ^ k)
            value = part[...]
            projected[pl.ds(pl.multiple_of(r * EDGE, EDGE), EDGE), :] = value
            turned[r] = value.T

    def add(col, product):
        for j in range(NY):
            total[col, j] += product[:, j * WIDTH : (j + 1) * WIDTH]

    def body(s, t, live):
        first = jnp.dot(turned[rows[s]], held[s], preferred_element_type=F32)
        second = jnp.dot(turned[rows[t]], held[t], preferred_element_type=F32)
        add(cols[s], first)
        add(cols[t], jnp.where(live, second, 0.0))

    over_slots(counts[0], body)
    for k in range(NZ):
        own[k] = total[z ^ k, y]
        for m in range(1, NY):
            sends[m - 1][k] = total[z ^ k, y ^ m].astype(BF16)


def backward(rows, cols, counts, held, mine, theirs):
    block = (NZ, WIDTH, WIDTH)
    return pl.pallas_call(
        backward_kernel,
        out_shape=(shape((ROWS * EDGE, WIDTH), BF16), shape(block, F32)) + (shape(block, BF16),) * (NY - 1),
        in_specs=[SMEM, SMEM, SMEM] + [VMEM] * (2 * NX + 1),
        out_specs=(VMEM,) * (NY + 1),
        scratch_shapes=[
            pltpu.VMEM((ROWS, WIDTH, EDGE), BF16),
            pltpu.VMEM((COLS, NY, WIDTH, WIDTH), F32),
        ],
        compiler_params=pltpu.CompilerParams(vmem_limit_bytes=24 << 20),
        name="backward",
    )(rows, cols, counts, held, *mine, *theirs)


def column_kernel(own, *refs):
    arrived, outs = refs[: NY - 1], refs[NY - 1 :]
    for k in range(NZ):
        value = own[k] + sum(r[k].astype(F32) for r in arrived)
        if k < 2:
            outs[0][k] = value
        else:
            outs[k // 2][k % 2] = value.astype(BF16)


def column_sum(own, arrived):
    block = (2, WIDTH, WIDTH)
    return pl.pallas_call(
        column_kernel,
        out_shape=(shape(block, F32),) + (shape(block, BF16),) * (NZ // 2 - 1),
        in_specs=[VMEM] * NY,
        out_specs=(VMEM,) * (NZ // 2),
        compiler_params=pltpu.CompilerParams(vmem_limit_bytes=8 << 20),
        name="column_sum",
    )(own, *arrived)


def near_kernel(own, *refs):
    arrived, (mine, send) = refs[:-2], refs[-2:]
    mine[...] = own[0] + sum(r[0].astype(F32) for r in arrived)
    send[...] = (own[1] + sum(r[1].astype(F32) for r in arrived)).astype(BF16)


def near_sum(own, arrived):
    block = (WIDTH, WIDTH)
    return pl.pallas_call(
        near_kernel,
        out_shape=(shape(block, F32), shape(block, BF16)),
        in_specs=[VMEM] * (NZ // 2),
        out_specs=(VMEM, VMEM),
        compiler_params=pltpu.CompilerParams(vmem_limit_bytes=4 << 20),
        name="near_sum",
    )(own, *arrived)


def last_kernel(scale, own, other, out):
    out[...] = (own[...] + other[...].astype(F32)).T * scale


def last_sum(own, other, scale):
    return pl.pallas_call(
        functools.partial(last_kernel, scale),
        out_shape=shape((WIDTH, WIDTH), F32),
        in_specs=[VMEM, VMEM],
        out_specs=VMEM,
        compiler_params=pltpu.CompilerParams(vmem_limit_bytes=4 << 20),
        name="last_sum",
    )(own, other)


def local(tiles, tile_row, tile_col, tile_count, sketch):
    tiles = tiles.reshape(SLOTS, EDGE, EDGE)
    rows, cols, counts = tile_row.reshape(SLOTS), tile_col.reshape(SLOTS), tile_count.reshape(1)
    held = fetch(counts, tiles)
    pair = jnp.stack([sketch, z_swap(sketch, 1)])
    along_z = jnp.concatenate([pair] + [z_swap(pair, k) for k in (2, 4, 6)])
    gathered = [along_z] + [y_swap(along_z, m) for m in range(1, NY)]
    keep, send = forward(rows, cols, counts, held, gathered)
    own, *sends = pair_sum(keep, core_swap(send))
    share = share_sum(own, [x_swap(v, k) for k, v in enumerate(sends, 1)])
    mine = [share] + [x_swap(share, k) for k in range(1, NX)]
    theirs = [core_swap(v) for v in mine]
    projected, own, *sends = backward(rows, cols, counts, held, mine, theirs)
    own, *sends = column_sum(own, [y_swap(v, m) for m, v in enumerate(sends, 1)])
    own, send = near_sum(own, [z_swap(v, 2 * k) for k, v in enumerate(sends, 1)])
    load = max(1, lax.axis_size("cells") * SLOTS // (2 * COLS))
    back = last_sum(own, z_swap(send, 1), 1.0 / math.sqrt(load))
    return projected, back


def solution(mesh):
    return jax.shard_map(
        local,
        mesh=mesh,
        in_specs=(
            P("cells", "genes", None, None, None),
            P("cells", "genes", None),
            P("cells", "genes", None),
            P("cells", "genes"),
            P(("genes", "cells"), None),
        ),
        out_specs=(P("cells", None), P(("genes", "cells"), None)),
        check_vma=False,
    )
```

```python
import functools
import math

import jax
import jax.numpy as jnp
from jax import lax
from jax.experimental import pallas as pl
from jax.experimental.pallas import tpu as pltpu
from jax.sharding import PartitionSpec as P


NZ, NY, NX, NC = 8, 4, 4, 2
SLOTS, EDGE, WIDTH, ROWS, COLS = 16, 512, 128, 8, 8
UNROLL, HALF = 8, NZ // 2
F32, BF16 = jnp.float32, jnp.bfloat16
VMEM = pl.BlockSpec(memory_space=pltpu.VMEM)
SMEM = pl.BlockSpec(memory_space=pltpu.SMEM)
HBM = pl.BlockSpec(memory_space=pl.ANY)


def where_am_i():
    cell, gene = lax.axis_index("cells"), lax.axis_index("genes")
    return cell // NY, cell % NY, gene // NC, gene % NC


def z_swap(v, k):
    return lax.ppermute(v, "cells", [(z * NY + y, (z ^ k) * NY + y) for z in range(NZ) for y in range(NY)])


def y_swap(v, k):
    return lax.ppermute(v, "cells", [(z * NY + y, z * NY + (y ^ k)) for z in range(NZ) for y in range(NY)])


def x_swap(v, k):
    return lax.ppermute(v, "genes", [(x * NC + c, (x ^ k) * NC + c) for x in range(NX) for c in range(NC)])


def core_swap(v):
    return lax.ppermute(v, "genes", [(x * NC + c, x * NC + 1 - c) for x in range(NX) for c in range(NC)])


def shape(dims, dtype):
    return jax.ShapeDtypeStruct(dims, dtype)


def fetch_kernel(counts, tiles, held, sems):
    count = counts[0]
    for go in (True, False):
        for s in range(SLOTS):
            @pl.when(s < count)
            def _():
                copy = pltpu.make_async_copy(tiles.at[s], held.at[s], sems.at[s])
                copy.start() if go else copy.wait()


def fetch(counts, tiles):
    return pl.pallas_call(
        fetch_kernel,
        out_shape=shape((SLOTS, EDGE, EDGE), BF16),
        in_specs=[SMEM, HBM],
        out_specs=VMEM,
        scratch_shapes=[pltpu.SemaphoreType.DMA((SLOTS,))],
        compiler_params=pltpu.CompilerParams(vmem_limit_bytes=12 << 20),
        name="fetch",
    )(counts, tiles)


def over_slots(count, body):
    def step(i, _):
        slots = [UNROLL * i + j for j in range(UNROLL)]
        body(slots, [s < count for s in slots])
        return 0

    lax.fori_loop(0, (count + UNROLL - 1) // UNROLL, step, 0)


def forward_kernel(rows, cols, counts, held, *refs):
    gathered, (keep, send, sketch, total) = refs[: 2 * NY], refs[2 * NY :]
    z, y, x, c = where_am_i()
    for m in range(NY):
        part = pl.ds(pl.multiple_of((y ^ m) * WIDTH, WIDTH), WIDTH)
        for k in range(NZ):
            sketch[z ^ k, part, :] = gathered[k // HALF * NY + m][k % HALF]
    total[...] = jnp.zeros_like(total)

    def body(slots, live):
        products = [jnp.dot(held[s], sketch[cols[s]], preferred_element_type=F32) for s in slots]
        for s, ok, product in zip(slots, live, products):
            total[rows[s]] += jnp.where(ok, product, 0.0)

    over_slots(counts[0], body)
    for k in range(NX):
        keep[k] = total[c * NX + (x ^ k)]
        send[k] = total[(1 - c) * NX + (x ^ k)].astype(BF16)


def forward(rows, cols, counts, held, gathered):
    return pl.pallas_call(
        forward_kernel,
        out_shape=(shape((NX, EDGE, WIDTH), F32), shape((NX, EDGE, WIDTH), BF16)),
        in_specs=[SMEM, SMEM, SMEM] + [VMEM] * (2 * NY + 1),
        out_specs=(VMEM, VMEM),
        scratch_shapes=[
            pltpu.VMEM((COLS, EDGE, WIDTH), BF16),
            pltpu.VMEM((ROWS, EDGE, WIDTH), F32),
        ],
        compiler_params=pltpu.CompilerParams(vmem_limit_bytes=24 << 20),
        name="forward",
    )(rows, cols, counts, held, *gathered)


def pair_kernel(keep, other, own, *sends):
    own[...] = keep[0] + other[0].astype(F32)
    for k, out in enumerate(sends, 1):
        out[...] = (keep[k] + other[k].astype(F32)).astype(BF16)


def pair_sum(keep, other):
    return pl.pallas_call(
        pair_kernel,
        out_shape=(shape((EDGE, WIDTH), F32),) + (shape((EDGE, WIDTH), BF16),) * (NX - 1),
        in_specs=[VMEM, VMEM],
        out_specs=(VMEM,) * NX,
        compiler_params=pltpu.CompilerParams(vmem_limit_bytes=8 << 20),
        name="pair_sum",
    )(keep, other)


def share_kernel(own, *refs):
    refs[-1][...] = (own[...] + sum(r[...].astype(F32) for r in refs[:-1])).astype(BF16)


def share_sum(own, arrived):
    return pl.pallas_call(
        share_kernel,
        out_shape=shape((EDGE, WIDTH), BF16),
        in_specs=[VMEM] * NX,
        out_specs=VMEM,
        compiler_params=pltpu.CompilerParams(vmem_limit_bytes=4 << 20),
        name="share_sum",
    )(own, *arrived)


def backward_kernel(rows, cols, counts, held, *refs):
    mine, theirs = refs[:NX], refs[NX : 2 * NX]
    projected, *halves, turned, total = refs[2 * NX :]
    z, y, x, c = where_am_i()
    total[...] = jnp.zeros_like(total)
    for k in range(NX):
        for core, part in ((c, mine[k]), (1 - c, theirs[k])):
            r = core * NX + (x ^ k)
            value = part[...]
            projected[pl.ds(pl.multiple_of(r * EDGE, EDGE), EDGE), :] = value
            turned[r] = value.T

    def body(slots, live):
        products = [jnp.dot(turned[rows[s]], held[s], preferred_element_type=F32) for s in slots]
        for s, ok, product in zip(slots, live, products):
            product, col = jnp.where(ok, product, 0.0), cols[s]
            for j in range(NY):
                total[col, j] += product[:, j * WIDTH : (j + 1) * WIDTH]

    over_slots(counts[0], body)
    for k in range(NZ):
        outs = halves[k // HALF * NY :]
        outs[0][k % HALF] = total[z ^ k, y]
        for m in range(1, NY):
            outs[m][k % HALF] = total[z ^ k, y ^ m].astype(BF16)


def backward(rows, cols, counts, held, mine, theirs):
    block = (HALF, WIDTH, WIDTH)
    half = (shape(block, F32),) + (shape(block, BF16),) * (NY - 1)
    return pl.pallas_call(
        backward_kernel,
        out_shape=(shape((ROWS * EDGE, WIDTH), BF16),) + half * 2,
        in_specs=[SMEM, SMEM, SMEM] + [VMEM] * (2 * NX + 1),
        out_specs=(VMEM,) * (2 * NY + 1),
        scratch_shapes=[
            pltpu.VMEM((ROWS, WIDTH, EDGE), BF16),
            pltpu.VMEM((COLS, NY, WIDTH, WIDTH), F32),
        ],
        compiler_params=pltpu.CompilerParams(vmem_limit_bytes=24 << 20),
        name="backward",
    )(rows, cols, counts, held, *mine, *theirs)


def column_kernel(own, *refs):
    arrived, outs = refs[: NY - 1], refs[NY - 1 :]
    for k in range(HALF):
        value = own[k] + sum(r[k].astype(F32) for r in arrived)
        outs[k // 2][k % 2] = value.astype(outs[k // 2].dtype)


def column_sum(own, arrived, first):
    block = (2, WIDTH, WIDTH)
    return pl.pallas_call(
        column_kernel,
        out_shape=(shape(block, first), shape(block, BF16)),
        in_specs=[VMEM] * NY,
        out_specs=(VMEM, VMEM),
        compiler_params=pltpu.CompilerParams(vmem_limit_bytes=8 << 20),
    )(own, *arrived)


def near_kernel(own, *refs):
    arrived, (mine, send) = refs[:-2], refs[-2:]
    mine[...] = own[0] + sum(r[0].astype(F32) for r in arrived)
    send[...] = (own[1] + sum(r[1].astype(F32) for r in arrived)).astype(BF16)


def near_sum(own, arrived):
    block = (WIDTH, WIDTH)
    return pl.pallas_call(
        near_kernel,
        out_shape=(shape(block, F32), shape(block, BF16)),
        in_specs=[VMEM] * (NZ // 2),
        out_specs=(VMEM, VMEM),
        compiler_params=pltpu.CompilerParams(vmem_limit_bytes=4 << 20),
        name="near_sum",
    )(own, *arrived)


def last_kernel(scale, own, other, out):
    out[...] = (own[...] + other[...].astype(F32)).T * scale


def last_sum(own, other, scale):
    return pl.pallas_call(
        functools.partial(last_kernel, scale),
        out_shape=shape((WIDTH, WIDTH), F32),
        in_specs=[VMEM, VMEM],
        out_specs=VMEM,
        compiler_params=pltpu.CompilerParams(vmem_limit_bytes=4 << 20),
        name="last_sum",
    )(own, other)


def join_kernel(*refs):
    at, out = 0, refs[-1]
    for ref in refs[:-1]:
        if len(ref.shape) == 2:
            out[at] = ref[...]
            at += 1
        else:
            out[at : at + ref.shape[0]] = ref[...]
            at += ref.shape[0]


def join(*parts):
    total = sum(1 if v.ndim == 2 else v.shape[0] for v in parts)
    return pl.pallas_call(
        join_kernel,
        out_shape=shape((total, WIDTH, WIDTH), BF16),
        in_specs=[VMEM] * len(parts),
        out_specs=VMEM,
        compiler_params=pltpu.CompilerParams(vmem_limit_bytes=4 << 20),
        name="join",
    )(*parts)


def whole(tiles, tile_row, tile_col, tile_count, sketch):
    tiles = tiles.reshape(SLOTS, EDGE, EDGE)
    rows, cols, counts = tile_row.reshape(SLOTS), tile_col.reshape(SLOTS), tile_count.reshape(1)
    held = fetch(counts, tiles)
    pair = join(sketch, z_swap(sketch, 1))
    near = join(pair, z_swap(pair, 2))
    far = join(z_swap(pair, 4), z_swap(pair, 6))
    gathered = [near] + [y_swap(near, m) for m in range(1, NY)]
    gathered += [far] + [y_swap(far, m) for m in range(1, NY)]
    keep, send = forward(rows, cols, counts, held, gathered)
    own, *sends = pair_sum(keep, core_swap(send))
    share = share_sum(own, [x_swap(v, k) for k, v in enumerate(sends, 1)])
    mine = [share] + [x_swap(share, k) for k in range(1, NX)]
    theirs = [core_swap(v) for v in mine]
    projected, *halves = backward(rows, cols, counts, held, mine, theirs)
    near, far = halves[:NY], halves[NY:]
    arrived = [y_swap(v, m) for m, v in enumerate(far[1:], 1)]
    send4, send6 = column_sum(far[0], arrived, BF16)
    arrived = [y_swap(v, m) for m, v in enumerate(near[1:], 1)]
    own, send2 = column_sum(near[0], arrived, F32)
    others = [z_swap(v, k) for v, k in ((send2, 2), (send4, 4), (send6, 6))]
    own, send = near_sum(own, others)
    load = max(1, lax.axis_size("cells") * SLOTS // (2 * COLS))
    back = last_sum(own, z_swap(send, 1), 1.0 / math.sqrt(load))
    return projected, back


def solution(mesh):
    return jax.shard_map(
        whole,
        mesh=mesh,
        in_specs=(
            P("cells", "genes", None, None, None),
            P("cells", "genes", None),
            P("cells", "genes", None),
            P("cells", "genes"),
            P(("genes", "cells"), None),
        ),
        out_specs=(P("cells", None), P(("genes", "cells"), None)),
        check_vma=False,
    )
```
